32 devices in a mesh: parts: 2 (over x), loop: 16 (over z, y, core).
Axes of the slice: x: 2, y: 2, z: 4, core: 2. Of those that a mesh axis runs over, the one named last changes fastest.
Arguments:
- classes: int32 [256], P(('parts', 'loop')), parts along dimension 0, may hold values from 0 to 2
- forward_field: bfloat16 [256, 512, 128], P(('parts', 'loop')), parts along dimension 0, may hold values from -6 to 6
- adjoint_source: bfloat16 [256, 512, 128], P(('parts', 'loop')), parts along dimension 0, may hold values from -6 to 6
- leaf_solve: bfloat16 [6, 2, 512, 512], P('parts'), parts along dimension 0, may hold values from -0.1875 to 0.1875
- leaf_lift: bfloat16 [6, 2, 512, 128], P('parts'), parts along dimension 0, may hold values from -0.375 to 0.375
- leaf_skeleton: bfloat16 [6, 2, 128, 512], P('parts'), parts along dimension 0, may hold values from -0.1875 to 0.1875
- block_merge: bfloat16 [16, 2, 128, 128], P('parts'), parts along dimension 0, may hold values from -0.125 to 0.125
- block_split: bfloat16 [16, 2, 128, 128], P('parts'), parts along dimension 0, may hold values from -0.375 to 0.375
- level_up: bfloat16 [8, 2, 128, 256], P('parts'), parts along dimension 0, may hold values from -0.25 to 0.25
- level_down: bfloat16 [8, 2, 256, 256], P('parts'), parts along dimension 0, may hold values from -0.25 to 0.25
- level_parent: bfloat16 [8, 2, 256, 128], P('parts'), parts along dimension 0, may hold values from -0.375 to 0.375
- root_solve: bfloat16 [4, 128, 128], P('parts'), parts along dimension 0, may hold values from -0.375 to 0.375
- rim_left: bfloat16 [6, 2, 128, 128], P('parts'), parts along dimension 0, may hold values from -0.375 to 0.375
- rim_right: bfloat16 [6, 2, 128, 128], P('parts'), parts along dimension 0, may hold values from -0.375 to 0.375
- shape_derivative: float32 [6, 2, 512], P('parts'), parts along dimension 0, may hold values from -6 to 6
- illum_angle: float32 [256], P('parts'), parts along dimension 0, may hold values from -3.140625 to 3.140625
- illum_weight: float32 [256], P('parts'), parts along dimension 0, may hold values from 0.3 to 3
- illum_ids: int32 [64], replicated, may hold values from 0 to 127
Outputs:
- adjoint: bfloat16 [256, 512, 128], P(('parts', 'loop')), parts along dimension 0
- gradient: float32 [256], P(('parts', 'loop')), parts along dimension 0
The draws below stay inside these ranges and needn't reach their ends.
There are 2 independent parts, one for each index of `parts`. The reference program is written for one: setup_inputs(seed, part) draws one part's arguments, and reference() takes and returns one part's arrays. A program takes and returns all parts, laid end to end along the dimension named above; an argument that names none is the same for every part. Nothing has to cross between parts.
Inputs may be any that keep to these rules, and one draw needn't show every extreme that they name: `illum_ids`: which of the 128 tabulated illuminations each adjoint belongs to.
All inputs are finite; a program needn't handle non-finite values.
Results may differ from the reference program's by a relative error of at most 0.007.
Values may be sent and summed in bfloat16 or wider, within the bound.
No kernel may reach another device: no remote copies, remote signals or barrier semaphores. Data moves between devices by JAX's collectives and lax.ppermute only.
A program may use at most 128 MiB of HBM per device.

```python
import math
import jax
import jax.numpy as jnp
from jax import lax

NODES = 512
RANK = 128
RIM = 128
M = 64
NCLASS = 3
NILLUM = 128
C_DEV = 8
CELLS = 128
LEVELS = 4


def plant(entries, own_key, low, top_value):
    shape = entries.shape
    spot = [jax.random.randint(jax.random.fold_in(own_key, axis), (), 0, shape[axis]) for axis in range(len(shape))]
    entries = entries.at[tuple(spot)].set(low)
    longest = shape.index(max(shape))
    spot[longest] = (spot[longest] + 1) % shape[longest]
    return entries.at[tuple(spot)].set(top_value)


def levels(own_key, extent, cuts, least, largest):
    level = 1.0
    for dim, shards_of in cuts:
        steps = jax.random.uniform(jax.random.fold_in(jax.random.fold_in(own_key, 6), dim), (shards_of,), jnp.float32, least / len(cuts), largest / len(cuts))
        level = level * jnp.repeat(jnp.exp(steps), extent[dim] // shards_of).reshape((-1,) + (1,) * (len(extent) - 1 - dim))
    return level


def centred(rng, dims, deviation, reach, shards=(), held_as=jnp.bfloat16):
    entries = jax.random.normal(rng, dims, jnp.float32) * deviation
    if len(shards) > 0:
        entries = levels(rng, dims, shards, -0.22, 0.18) * entries
    return jnp.clip(entries, min=-reach, max=reach).astype(held_as)


def setup_inputs(seed: int = 0, part: int = 0) -> dict:
    keys = jax.random.split(jax.random.key(seed), 19)
    own_keys = jax.random.split(jax.random.fold_in(keys[18], part), 19)
    classes = plant(jax.random.randint(own_keys[0], (CELLS,), 0, NCLASS), jax.random.fold_in(own_keys[0], 1), 0, NCLASS - 1).astype(jnp.int32)
    forward_field = centred(own_keys[1], (CELLS, NODES, 2 * M), 1.0, 6.0, ((0, 16),))
    adjoint_source = centred(own_keys[2], (CELLS, NODES, 2 * M), 1.0, 6.0, ((0, 16),))
    leaf_solve = centred(own_keys[3], (NCLASS, 2, NODES, NODES), (2 * NODES) ** -0.5, 0.1875)
    leaf_lift = centred(own_keys[4], (NCLASS, 2, NODES, RANK), (2 * RANK) ** -0.5, 0.375)
    leaf_skeleton = centred(own_keys[5], (NCLASS, 2, RANK, NODES), (2 * NODES) ** -0.5, 0.1875)
    block_merge = centred(own_keys[6], (C_DEV, 2, RANK, RANK), (2 * RANK * C_DEV) ** -0.5, 0.125)
    block_split = centred(own_keys[7], (C_DEV, 2, RANK, RANK), (2 * RANK) ** -0.5, 0.375)
    level_up = centred(own_keys[8], (LEVELS, 2, RANK, 2 * RANK), (4 * RANK) ** -0.5, 0.25)
    level_down = centred(own_keys[9], (LEVELS, 2, 2 * RANK, 2 * RANK), (4 * RANK) ** -0.5, 0.25)
    level_parent = centred(own_keys[10], (LEVELS, 2, 2 * RANK, RANK), (2 * RANK) ** -0.5, 0.375)
    root_solve = centred(own_keys[11], (2, RANK, RANK), (2 * RANK) ** -0.5, 0.375)
    rim_left = centred(own_keys[12], (NCLASS, 2, RIM, RIM), (2 * RIM) ** -0.5, 0.375)
    rim_right = centred(own_keys[13], (NCLASS, 2, RIM, RIM), (2 * RIM) ** -0.5, 0.375)
    shape_derivative = centred(own_keys[14], (NCLASS, 2, NODES), 1.0, 6.0, (), jnp.float32)
    illum_angle = jnp.clip(jax.random.uniform(own_keys[15], (NILLUM,), jnp.float32, -3.140625, 3.140625), -3.140625, 3.140625)
    illum_weight = jnp.clip(jnp.exp(jax.random.uniform(own_keys[16], (NILLUM,), jnp.float32, math.log(0.3), math.log(3.0))), 0.3, 3.0)
    illum_ids = plant(jax.random.randint(keys[17], (M,), 0, NILLUM), jax.random.fold_in(keys[17], 1), 0, NILLUM - 1).astype(jnp.int32)
    return dict(classes=classes, forward_field=forward_field, adjoint_source=adjoint_source, leaf_solve=leaf_solve, leaf_lift=leaf_lift, leaf_skeleton=leaf_skeleton, block_merge=block_merge, block_split=block_split, level_up=level_up, level_down=level_down, level_parent=level_parent, root_solve=root_solve, rim_left=rim_left, rim_right=rim_right, shape_derivative=shape_derivative, illum_angle=illum_angle, illum_weight=illum_weight, illum_ids=illum_ids)


PRECISE = lax.Precision.HIGHEST

def rotate_half(values):
    middle = values.shape[-1] // 2
    return jnp.concatenate([-values[..., middle:], values[..., :middle]], axis=-1)

def complex_product(matrix, block):
    direct = jnp.dot(matrix[0], block, preferred_element_type=jnp.float32)
    twisted = jnp.dot(matrix[1], block, preferred_element_type=jnp.float32)
    return direct + rotate_half(twisted)

def complex_exact(matrix, block):
    wide = matrix.astype(jnp.float32)
    direct = jnp.dot(wide[0], block, precision=PRECISE, preferred_element_type=jnp.float32)
    twisted = jnp.dot(wide[1], block, precision=PRECISE, preferred_element_type=jnp.float32)
    return direct + rotate_half(twisted)

def phase_turn(values, cosine, sine_values):
    middle = values.shape[-1] // 2
    real_part = values[..., :middle]
    imag_part = values[..., middle:]
    return jnp.concatenate([real_part * cosine - imag_part * sine_values, real_part * sine_values + imag_part * cosine], axis=-1)

def reference(classes, forward_field, adjoint_source, leaf_solve, leaf_lift, leaf_skeleton, block_merge, block_split, level_up, level_down, level_parent, root_solve, rim_left, rim_right, shape_derivative, illum_angle, illum_weight, illum_ids):
    cell_count = classes.shape[0]
    block_cells = block_merge.shape[0]
    block_count = cell_count // block_cells
    rank = root_solve.shape[-1]
    width = forward_field.shape[-1]
    illum = width // 2
    nodes = forward_field.shape[1]
    rim = rim_left.shape[-1]

    def leaf_up(element):
        return complex_product(leaf_skeleton[element[0]], element[1])
    skeleton_cells = lax.map(leaf_up, (classes, adjoint_source))
    grouped = skeleton_cells.reshape(block_count, block_cells, rank, width)
    merge_wide = block_merge.astype(jnp.float32)
    block_source = jnp.einsum('prc,dpck->drk', merge_wide[:, 0], grouped, precision=PRECISE) + rotate_half(jnp.einsum('prc,dpck->drk', merge_wide[:, 1], grouped, precision=PRECISE))
    stored = []
    nodes_now = block_source
    for level in range(level_up.shape[0]):
        count = nodes_now.shape[0] // 2
        sibling_pairs = nodes_now.reshape(count, 2 * rank, width)
        stored.append(sibling_pairs)
        nodes_now = jax.vmap(complex_exact, in_axes=(None, 0))(level_up[level], sibling_pairs)
    fields = complex_exact(root_solve, nodes_now[0])[None]
    for level in reversed(range(level_up.shape[0])):
        children = jax.vmap(complex_exact, in_axes=(None, 0))(level_down[level], stored[level]) + jax.vmap(complex_exact, in_axes=(None, 0))(level_parent[level], fields)
        fields = children.reshape(2 * children.shape[0], rank, width)
    split_wide = block_split.astype(jnp.float32)
    cell_field = jnp.einsum('prc,dck->dprk', split_wide[:, 0], fields, precision=PRECISE) + rotate_half(jnp.einsum('prc,dck->dprk', split_wide[:, 1], fields, precision=PRECISE))
    cell_field = cell_field.reshape(cell_count, rank, width).astype(jnp.bfloat16)

    def leaf_down(element):
        geometry, source, lifted = element
        return (complex_product(leaf_solve[geometry], source) + complex_product(leaf_lift[geometry], lifted)).astype(jnp.bfloat16)
    adjoint = lax.map(leaf_down, (classes, adjoint_source, cell_field))
    angles = illum_angle[illum_ids]
    weights = illum_weight[illum_ids]
    cosine = jnp.cos(angles)
    sine_values = jnp.sin(angles)
    left_in = jnp.roll(forward_field[:, nodes - rim:], 1, axis=0)
    right_in = jnp.roll(forward_field[:, :rim], -1, axis=0)
    left_term = lax.map(lambda element: complex_product(rim_left[element[0]], element[1]), (classes, left_in))
    right_term = lax.map(lambda element: complex_product(rim_right[element[0]], element[1]), (classes, right_in))
    left_term = left_term.at[0].set(phase_turn(left_term[0], cosine, -sine_values))
    right_term = right_term.at[cell_count - 1].set(phase_turn(right_term[cell_count - 1], cosine, sine_values))
    derivative = shape_derivative[classes]
    field_wide = forward_field.astype(jnp.float32)
    real_part = field_wide[..., :illum]
    imag_part = field_wide[..., illum:]
    deriv_real = derivative[:, 0, :, None]
    deriv_imag = derivative[:, 1, :, None]
    perturbed = jnp.concatenate([deriv_real * real_part - deriv_imag * imag_part, deriv_real * imag_part + deriv_imag * real_part], axis=-1)
    perturbed = jnp.concatenate([perturbed[:, :rim] + left_term, perturbed[:, rim:nodes - rim], perturbed[:, nodes - rim:] + right_term], axis=1)
    adjoint_wide = adjoint.astype(jnp.float32)
    pointwise = adjoint_wide[..., :illum] * perturbed[..., :illum] - adjoint_wide[..., illum:] * perturbed[..., illum:]
    gradient = jnp.dot(lax.optimization_barrier(jnp.sum(pointwise, axis=1)), weights, precision=PRECISE) / math.sqrt(NODES * M)
    return (adjoint, gradient)
```

```python
import functools
import math

import jax
import jax.numpy as jnp
from jax import lax
from jax.experimental import pallas as pl
from jax.experimental.pallas import tpu as pltpu
from jax.sharding import PartitionSpec as P

F32 = jnp.float32
BF16 = jnp.bfloat16
MIB = 1 << 20
VM = pl.BlockSpec(memory_space=pltpu.VMEM)
SM = pl.BlockSpec(memory_space=pltpu.SMEM)
ANY = pl.BlockSpec(memory_space=pl.ANY)


def params(mib):
    return pltpu.CompilerParams(vmem_limit_bytes=mib * MIB)


def cost(flops, nbytes):
    return pl.CostEstimate(flops=flops, bytes_accessed=nbytes, transcendentals=0)


def half_sign(width):
    lane = lax.broadcasted_iota(jnp.int32, (1, width), 1)
    return jnp.where(lane < width // 2, -1.0, 1.0).astype(F32)


def turn(values):
    width = values.shape[-1]
    return pltpu.roll(values, width // 2, 1) * half_sign(width)


def dot(a, b):
    return jnp.dot(a, b, preferred_element_type=F32)


def split(x):
    high = x.astype(BF16)
    return high, (x - high.astype(F32)).astype(BF16)


def embed(re, im):
    return jnp.concatenate(
        [jnp.concatenate([re, -im], axis=1), jnp.concatenate([im, re], axis=1)], axis=0
    )


def times(re, im, stacked):
    left = embed(re, im)
    if stacked.dtype == BF16:
        return dot(left, stacked)
    high, low = split(stacked)
    return dot(left, high) + dot(left, low)


def side_by_side(stacked):
    rows = stacked.shape[0] // 2
    return jnp.concatenate([stacked[:rows], stacked[rows:]], axis=1)


def groups_of(levels):
    return [tuple(range(low, min(low + 2, levels))) for low in range(0, levels, 2)]


def pair_of(ref, level):
    return ref[level, 0], ref[level, 1]


def up_map(group, up_ref, left_of):
    rank = up_ref.shape[2]
    bottom = jnp.concatenate([up_ref[group[0], 0], up_ref[group[0], 1]], axis=0)
    re, im = left_of
    return jnp.concatenate(
        [
            times(re[:, j * rank : (j + 1) * rank], im[:, j * rank : (j + 1) * rank], bottom)
            for j in range(2)
        ],
        axis=1,
    )


def rows_of(ref, level, bit):
    rank = ref.shape[2] // 2
    start = pl.multiple_of(bit * rank, rank)
    return ref[level, 0, pl.ds(start, rank), :], ref[level, 1, pl.ds(start, rank), :]


def group_maps(group, position, up_ref, down_ref, parent_ref):
    low = group[0]
    low_bit = (position >> low) & 1
    parent_re, parent_im = rows_of(parent_ref, low, low_bit)
    down_re, down_im = rows_of(down_ref, low, low_bit)
    local = jnp.concatenate([down_re, down_im], axis=0).astype(F32)
    if len(group) == 1:
        up = jnp.concatenate([up_ref[low, 0], up_ref[low, 1]], axis=0)
        return up.astype(F32), local, jnp.concatenate([parent_re, parent_im], axis=0).astype(F32)
    high = group[1]
    high_bit = (position >> high) & 1
    w = up_map(group, up_ref, pair_of(up_ref, high))
    inner = up_map(group, up_ref, rows_of(down_ref, high, high_bit))
    outer = times(parent_re, parent_im, inner)
    placed = jnp.concatenate(
        [
            local * jnp.where(high_bit == 0, 1.0, 0.0).astype(F32),
            local * jnp.where(high_bit == 1, 1.0, 0.0).astype(F32),
        ],
        axis=1,
    )
    top_re, top_im = rows_of(parent_ref, high, high_bit)
    q = times(parent_re, parent_im, jnp.concatenate([top_re, top_im], axis=0))
    return w, outer + placed, q


def up_kernel(scal, source, skeleton, merge, forward, out, even, odd, src_v, skel_v, merge_v, sems):
    cells = src_v.shape[0]
    classes = skel_v.shape[0]
    rim = even.shape[0]
    nodes = forward.shape[1]
    parity = scal[cells] & 1
    copies = []

    def start(src, dst, i):
        c = pltpu.make_async_copy(src, dst, sems.at[i])
        c.start()
        copies.append(c)

    for k in range(classes):
        start(skeleton.at[k], skel_v.at[k], k)
    for p in range(cells):
        start(source.at[p], src_v.at[p], classes + p)
    start(merge, merge_v, classes + cells)
    last = (cells - 1, nodes - rim)
    even_cell = jnp.where(parity == 0, last[0], 0)
    even_row = pl.multiple_of(jnp.where(parity == 0, last[1], 0), rim)
    odd_cell = jnp.where(parity == 1, last[0], 0)
    odd_row = pl.multiple_of(jnp.where(parity == 1, last[1], 0), rim)
    start(forward.at[even_cell, pl.ds(even_row, rim), :], even, classes + cells + 1)
    start(forward.at[odd_cell, pl.ds(odd_row, rim), :], odd, classes + cells + 2)
    for k in range(classes):
        copies[k].wait()
    pieces = []
    for p in range(cells):
        copies[classes + p].wait()
        k = scal[p]
        v = src_v[p]
        weights = jnp.concatenate([skel_v[k, 0], skel_v[k, 1]], axis=0)
        rank = skel_v.shape[2]
        both = dot(weights, v)
        pieces.append((both[:rank] + turn(both[rank:])).astype(BF16))
    copies[classes + cells].wait()
    total = None
    rank = skel_v.shape[2]
    for p in range(0, cells, 2):
        mine = range(p, min(p + 2, cells))
        left = jnp.concatenate(
            [
                jnp.concatenate([merge_v[i, 0] for i in mine], axis=1),
                jnp.concatenate([merge_v[i, 1] for i in mine], axis=1),
            ],
            axis=0,
        )
        term = dot(left, jnp.concatenate([pieces[i] for i in mine], axis=0))
        total = term if total is None else total + term
    out[...] = (total[:rank] + turn(total[rank:])).astype(BF16)
    copies[classes + cells + 1].wait()
    copies[classes + cells + 2].wait()


def local_kernel(scal, source, solve, up_ref, down_ref, parent_ref, _, local, maps, *, groups):
    cells = source.shape[0]
    position = scal[cells]
    rank = up_ref.shape[2]
    for g, group in enumerate(groups[:-1]):
        w, f, _q = group_maps(group, position, up_ref, down_ref, parent_ref)
        columns = 2 * w.shape[1]
        maps[g, :rank, :columns] = side_by_side(w).astype(BF16)
        maps[g, rank:, :columns] = side_by_side(f).astype(BF16)

    @pl.loop(0, cells)
    def _loop(p):
        k = scal[p]
        v = source[p]
        turned = turn(v.astype(F32)).astype(BF16)
        left = jnp.concatenate([solve[k, 0], solve[k, 1]], axis=1)
        local[p] = dot(left, jnp.concatenate([v, turned], axis=0))


def gather_nodes(group, position, own, arrived, nodes_v):
    count = 1 << len(group)
    rank = own.shape[0]
    index = (position >> group[0]) & (count - 1)
    for mask in range(count):
        value = own[...] if mask == 0 else arrived[mask - 1][...]
        where = index ^ mask
        nodes_v[where] = value
        nodes_v[count + where] = turn(value.astype(F32)).astype(BF16)
    return nodes_v[: 2 * count].reshape(2 * count * rank, own.shape[1])


def combine_kernel(scal, maps, own, *refs, group, index, cells):
    count = 1 << len(group)
    arrived = refs[: count - 1]
    node, part, nodes_v = refs[count - 1 :]
    rank = own.shape[0]
    stack = gather_nodes(group, scal[cells], own, arrived, nodes_v)
    both = dot(maps[index, :, : stack.shape[0]], stack)
    node[...] = both[:rank].astype(BF16)
    part[...] = both[rank:]


def perturb_kernel(
    scal,
    forward,
    even,
    odd,
    rim_left,
    rim_right,
    shape_ref,
    angle_ref,
    weight_ref,
    ids_ref,
    up_ref,
    down_ref,
    parent_ref,
    root_ref,
    _,
    weighted,
    final_map,
    columns,
    *,
    groups,
    device_count,
):
    cells, nodes, width = forward.shape
    rim = even.shape[0]
    classes = shape_ref.shape[0]
    position = scal[cells]
    parity = position & 1

    w, f, q = group_maps(groups[-1], position, up_ref, down_ref, parent_ref)
    top = times(root_ref[0], root_ref[1], w)
    rank = root_ref.shape[1]
    high, low = split(q)
    top_high, top_low = split(top)
    left = embed(high[:rank], high[rank:])
    extra = embed(low[:rank], low[rank:])
    total = f + dot(left, top_high) + dot(left, top_low) + dot(extra, top_high)
    for group in reversed(groups[:-1]):
        for level in reversed(group):
            re, im = rows_of(parent_ref, level, (position >> level) & 1)
            total = times(re, im, total)
    final_map[...] = side_by_side(total).astype(BF16)

    ids = jnp.concatenate([ids_ref[...], ids_ref[...]], axis=1)
    table = angle_ref.shape[1]
    chosen = lax.broadcasted_iota(jnp.int32, (table, width), 0) == ids

    def column_of(row):
        return jnp.transpose(jnp.broadcast_to(row, (8, table)))[:, :1]

    angles = jnp.sum(jnp.where(chosen, column_of(angle_ref[...]), 0.0), axis=0, keepdims=True)
    weights = jnp.sum(jnp.where(chosen, column_of(weight_ref[...]), 0.0), axis=0, keepdims=True)
    weights = weights * half_sign(width) * (-1.0 / math.sqrt(nodes * (width // 2)))
    cosine = jnp.cos(angles)
    sine = jnp.sin(angles)

    for k in range(classes):
        turned = jnp.transpose(jnp.concatenate([shape_ref[k]] * 4, axis=0))
        columns[k, 0] = jnp.broadcast_to(turned[:, 0:1], (nodes, width)) * weights
        columns[k, 1] = jnp.broadcast_to(turned[:, 1:2], (nodes, width)) * weights

    def rim_term(ref, k, block):
        both = dot(jnp.concatenate([ref[k, 0], ref[k, 1]], axis=0), block)
        return both[:rim] + turn(both[rim:])

    def phase_turn(values, active, sign):
        c = jnp.where(active, cosine, 1.0)
        s = jnp.where(active, sine * sign, 0.0)
        return values * c + turn(values) * s

    before = jnp.where(parity == 1, even[...], odd[...])
    after = jnp.where(parity == 0, even[...], odd[...])
    for p in range(cells):
        k = scal[p]
        field = forward[p].astype(F32)
        value = columns[k, 0] * field + columns[k, 1] * turn(field)
        left_in = before if p == 0 else forward[p - 1, nodes - rim :, :]
        right_in = after if p == cells - 1 else forward[p + 1, :rim, :]
        left_term = rim_term(rim_left, k, left_in)
        right_term = rim_term(rim_right, k, right_in)
        if p == 0:
            left_term = phase_turn(left_term, position == 0, -1.0)
        if p == cells - 1:
            right_term = phase_turn(right_term, position == device_count - 1, 1.0)
        weighted[p, :rim, :] = value[:rim] + left_term * weights
        weighted[p, rim : nodes - rim, :] = value[rim : nodes - rim]
        weighted[p, nodes - rim :, :] = value[nodes - rim :] + right_term * weights


def down_kernel(scal, final_map, own, *refs, group, cells):
    count = 1 << len(group)
    arrived = refs[: count - 1]
    part, split_ref, lift, local, weighted, adjoint, gradient, nodes_v, out_v, sems = refs[count - 1 :]
    rank = own.shape[0]
    width = own.shape[1]
    stack = gather_nodes(group, scal[cells], own, arrived, nodes_v)
    field = dot(final_map[...], stack) + part[...]
    both = jnp.concatenate([field.astype(BF16), turn(field).astype(BF16)], axis=0)
    copies = []
    sums = []
    for p in range(cells):
        k = scal[p]
        cell = dot(jnp.concatenate([split_ref[p, 0], split_ref[p, 1]], axis=1), both)
        rhs = jnp.concatenate([cell.astype(BF16), turn(cell).astype(BF16)], axis=0)
        value = local[p] + dot(jnp.concatenate([lift[k, 0], lift[k, 1]], axis=1), rhs)
        rounded = value.astype(BF16)
        out_v[p] = rounded
        c = pltpu.make_async_copy(out_v.at[p], adjoint.at[p], sems.at[p])
        c.start()
        copies.append(c)
        sums.append(jnp.sum(rounded.astype(F32) * weighted[p], axis=0, keepdims=True))
    table = jnp.sum(jnp.concatenate(sums, axis=0), axis=1, keepdims=True)
    row = lax.broadcasted_iota(jnp.int32, (cells, cells), 0)
    lane = lax.broadcasted_iota(jnp.int32, (cells, cells), 1)
    gradient[...] = jnp.sum(jnp.where(row == lane, table, 0.0), axis=0, keepdims=True)
    for c in copies:
        c.wait()


def shards(
    classes,
    forward_field,
    adjoint_source,
    leaf_solve,
    leaf_lift,
    leaf_skeleton,
    block_merge,
    block_split,
    level_up,
    level_down,
    level_parent,
    root_solve,
    rim_left,
    rim_right,
    shape_derivative,
    illum_angle,
    illum_weight,
    illum_ids,
):
    position = lax.axis_index("loop")
    device_count = lax.axis_size("loop")
    cells, nodes, width = adjoint_source.shape
    class_count = leaf_solve.shape[0]
    rank = root_solve.shape[-1]
    rim = rim_left.shape[-1]
    levels = level_up.shape[0]
    groups = groups_of(levels)
    scal = jnp.concatenate([classes, position.astype(jnp.int32)[None]])
    sds = jax.ShapeDtypeStruct
    node = sds((rank, width), BF16)

    source, even, odd = pl.pallas_call(
        up_kernel,
        out_shape=(node, sds((rim, width), BF16), sds((rim, width), BF16)),
        in_specs=[SM, ANY, ANY, ANY, ANY],
        out_specs=(VM, VM, VM),
        scratch_shapes=[
            pltpu.VMEM((cells, nodes, width), BF16),
            pltpu.VMEM((class_count, 2, rank, nodes), BF16),
            pltpu.VMEM(block_merge.shape, BF16),
            pltpu.SemaphoreType.DMA((class_count + cells + 3,)),
        ],
        compiler_params=params(12),
        cost_estimate=cost(4 * cells * rank * nodes * width, 3 * MIB),
        name="up",
    )(scal, adjoint_source, leaf_skeleton, block_merge, forward_field)

    def exchange(value, mask):
        pairs = [(i, i ^ mask) for i in range(device_count)]
        return lax.ppermute(value, "loop", pairs)

    def odd_exchange(value):
        pairs = [
            (i, (i + 1) % device_count if i % 2 else (i - 1) % device_count)
            for i in range(device_count)
        ]
        return lax.ppermute(value, "loop", pairs)

    def gather(value, group):
        base = 1 << group[0]
        return [exchange(value, base * m) for m in range(1, 1 << len(group))]

    even_in = exchange(even, 1)
    arrived = gather(source, groups[0])
    odd_in = odd_exchange(odd)

    most = 2 * (rank << 2)
    local, maps = pl.pallas_call(
        functools.partial(local_kernel, groups=groups),
        out_shape=(
            sds((cells, nodes, width), F32),
            sds((max(len(groups) - 1, 1), 2 * rank, most), BF16),
        ),
        in_specs=[SM] + [VM] * 6,
        out_specs=(VM, VM),
        compiler_params=params(8),
        cost_estimate=cost(8 * cells * nodes * nodes * width, 6 * MIB),
        name="local",
    )(scal, adjoint_source, leaf_solve, level_up, level_down, level_parent, source)

    own = source
    fields = []
    for g, group in enumerate(groups[:-1]):
        count = 1 << len(group)
        own, part = pl.pallas_call(
            functools.partial(combine_kernel, group=group, index=g, cells=cells),
            out_shape=(node, sds((rank, width), F32)),
            in_specs=[SM] + [VM] * (1 + count),
            out_specs=(VM, VM),
            scratch_shapes=[pltpu.VMEM((2 * count, rank, width), BF16)],
            compiler_params=params(4),
            cost_estimate=cost(16 * rank * rank * width, MIB),
            name="combine",
        )(scal, maps, own, *arrived)
        fields.append((group, part))
        arrived = gather(own, groups[g + 1])

    weighted, final_map = pl.pallas_call(
        functools.partial(perturb_kernel, groups=groups, device_count=device_count),
        out_shape=(
            sds((cells, nodes, width), F32),
            sds((rank, 2 * (rank << len(groups[-1]))), BF16),
        ),
        in_specs=[SM] + [VM] * 14,
        out_specs=(VM, VM),
        scratch_shapes=[pltpu.VMEM((class_count, 2, nodes, width), F32)],
        compiler_params=params(10),
        cost_estimate=cost(8 * cells * rim * rim * width, 4 * MIB),
        name="perturb",
    )(
        scal,
        forward_field,
        even_in,
        odd_in,
        rim_left,
        rim_right,
        shape_derivative,
        illum_angle[None],
        illum_weight[None],
        illum_ids[None],
        level_up,
        level_down,
        level_parent,
        root_solve,
        own,
    )

    part = fold_parts(fields, level_parent, position, rank, width)
    group = groups[-1]
    count = 1 << len(group)
    adjoint, gradient = pl.pallas_call(
        functools.partial(down_kernel, group=group, cells=cells),
        out_shape=(sds((cells, nodes, width), BF16), sds((1, cells), F32)),
        in_specs=[SM] + [VM] * (count + 1 + 5),
        out_specs=(ANY, VM),
        scratch_shapes=[
            pltpu.VMEM((2 * count, rank, width), BF16),
            pltpu.VMEM((cells, nodes, width), BF16),
            pltpu.SemaphoreType.DMA((cells,)),
        ],
        compiler_params=params(8),
        cost_estimate=cost(8 * cells * nodes * rank * width, 8 * MIB),
        name="down",
    )(scal, final_map, own, *arrived, part, block_split, leaf_lift, local, weighted)
    return adjoint, gradient[0]


def fold_parts(fields, level_parent, position, rank, width):
    if not fields:
        return jnp.zeros((rank, width), F32)
    total = fields[-1][1]
    for group, part in reversed(fields[:-1]):
        for level in reversed(group):
            start = ((position >> level) & 1) * rank
            rows = lax.dynamic_slice_in_dim(level_parent[level], start, rank, 1).astype(F32)
            direct = jnp.dot(rows[0], total, precision=lax.Precision.HIGHEST)
            twisted = jnp.dot(rows[1], total, precision=lax.Precision.HIGHEST)
            half = width // 2
            total = direct + jnp.concatenate([-twisted[:, half:], twisted[:, :half]], axis=1)
        total = total + part
    return total


def solution(mesh):
    return jax.shard_map(
        shards,
        mesh=mesh,
        in_specs=(
            P(("parts", "loop")),
            P(("parts", "loop"), None, None),
            P(("parts", "loop"), None, None),
            P("parts", None, None, None),
            P("parts", None, None, None),
            P("parts", None, None, None),
            P("parts", None, None, None),
            P("parts", None, None, None),
            P("parts", None, None, None),
            P("parts", None, None, None),
            P("parts", None, None, None),
            P("parts", None, None),
            P("parts", None, None, None),
            P("parts", None, None, None),
            P("parts", None, None),
            P("parts"),
            P("parts"),
            P(),
        ),
        out_specs=(P(("parts", "loop"), None, None), P(("parts", "loop"))),
        check_vma=False,
    )
```

```python
import functools
import math

import jax
import jax.numpy as jnp
from jax import lax
from jax.experimental import pallas as pl
from jax.experimental.pallas import tpu as pltpu
from jax.sharding import PartitionSpec as P

F32 = jnp.float32
BF16 = jnp.bfloat16
MIB = 1 << 20
VM = pl.BlockSpec(memory_space=pltpu.VMEM)
HBM = pl.BlockSpec(memory_space=pltpu.HBM)


def params(mib):
    return pltpu.CompilerParams(vmem_limit_bytes=mib * MIB)


def cost(flops, nbytes):
    return pl.CostEstimate(flops=flops, bytes_accessed=nbytes, transcendentals=0)


def half_sign(width):
    lane = lax.broadcasted_iota(jnp.int32, (1, width), 1)
    return jnp.where(lane < width // 2, -1.0, 1.0).astype(F32)


def turn(values):
    width = values.shape[-1]
    return pltpu.roll(values, width // 2, 1) * half_sign(width)


def dot(a, b):
    return jnp.dot(a, b, preferred_element_type=F32)


def split(x):
    high = x.astype(BF16)
    return high, (x - high.astype(F32)).astype(BF16)


def embed(re, im):
    return jnp.concatenate(
        [jnp.concatenate([re, -im], axis=1), jnp.concatenate([im, re], axis=1)], axis=0
    )


def times(re, im, stacked):
    left = embed(re, im)
    if stacked.dtype == BF16:
        return dot(left, stacked)
    high, low = split(stacked)
    return dot(left, high) + dot(left, low)


def side_by_side(stacked):
    rows = stacked.shape[0] // 2
    return jnp.concatenate([stacked[:rows], stacked[rows:]], axis=1)


def groups_of(levels):
    return [tuple(range(low, min(low + 2, levels))) for low in range(0, levels, 2)]


def wide(ref, *at):
    return jnp.concatenate([ref[(*at, 0)], ref[(*at, 1)]], axis=1)


def tall(ref, *at):
    return jnp.concatenate([ref[(*at, 0)], ref[(*at, 1)]], axis=0)


def rows_of(ref, level, bit):
    rank = ref.shape[2] // 2
    start = pl.multiple_of(bit * rank, rank)
    return ref[level, 0, pl.ds(start, rank), :], ref[level, 1, pl.ds(start, rank), :]


def turned(value):
    return turn(value.astype(F32)).astype(BF16)


def slot_count(cells, classes):
    return (cells + classes) // 2


def table_size(slots):
    return -(-(3 * slots + 3) // 128) * 128


class Pairs:
    def __init__(self, table, slots):
        self.table, self.slots = table, slots

    def ends(self):
        return self.table[3 * self.slots + 1], self.table[3 * self.slots + 2]

    def __getitem__(self, slot):
        return tuple(self.table[i * self.slots + slot] for i in range(3))

    def used(self):
        return self.table[3 * self.slots]


def fill_pairs(scal, table, cells, classes):
    slots = slot_count(cells, classes)
    slot = jnp.int32(0)
    for k in range(classes):
        half = jnp.int32(0)
        for p in range(cells):
            mine = scal[p] == k

            @pl.when(jnp.logical_and(mine, half == 0))
            def _first(k=k, p=p, slot=slot):
                table[slot] = k
                table[slots + slot] = p

            @pl.when(mine)
            def _second(p=p, slot=slot):
                table[2 * slots + slot] = p

            step = mine.astype(jnp.int32)
            slot = slot + step * half
            half = jnp.where(mine, 1 - half, half)
        slot = slot + half
    table[3 * slots] = slot
    table[3 * slots + 1] = scal[0]
    table[3 * slots + 2] = scal[cells - 1]
    for s in range((cells + 1) // 2, slots):

        @pl.when(s >= slot)
        def _spare(s=s):
            for i in range(3):
                table[i * slots + s] = table[i * slots]


def up_kernel(
    classes_h,
    source,
    skeleton,
    merge,
    forward,
    out,
    joint,
    odd,
    table_out,
    scal,
    table,
    src_v,
    skel_v,
    merge_v,
    cell_v,
    sems,
):
    cells, nodes, width = src_v.shape
    classes = skel_v.shape[0]
    rank = skel_v.shape[2]
    rim = odd.shape[0]
    parity = lax.axis_index("loop") & 1
    copies = []

    def start(src, dst, i):
        c = pltpu.make_async_copy(src, dst, sems.at[i])
        c.start()
        copies.append(c)

    start(classes_h, scal, 0)
    start(skeleton, skel_v, 1)
    start(source, src_v, 2)
    start(merge, merge_v, 3)
    last = (cells - 1, nodes - rim)
    even_cell = jnp.where(parity == 0, last[0], 0)
    even_row = pl.multiple_of(jnp.where(parity == 0, last[1], 0), rim)
    odd_cell = jnp.where(parity == 1, last[0], 0)
    odd_row = pl.multiple_of(jnp.where(parity == 1, last[1], 0), rim)
    start(forward.at[even_cell, pl.ds(even_row, rim), :], joint.at[pl.ds(rank, rim), :], 4)
    start(forward.at[odd_cell, pl.ds(odd_row, rim), :], odd, 5)
    copies[0].wait()
    fill_pairs(scal, table, cells, classes)
    start(table, table_out, 6)
    slots = slot_count(cells, classes)
    pairs = Pairs(table, slots)
    copies[1].wait()
    copies[2].wait()
    for s in range(slots):
        k, a, b = pairs[s]
        both = dot(tall(skel_v, k), jnp.concatenate([src_v[a], src_v[b]], axis=1))
        for i, p in enumerate((a, b)):
            part = both[:, i * width : (i + 1) * width]
            cell_v[p] = (part[:rank] + turn(part[rank:])).astype(BF16)
    copies[3].wait()
    total = None
    for p in range(0, cells, 2):
        mine = range(p, min(p + 2, cells))
        left = jnp.concatenate(
            [jnp.concatenate([merge_v[i, part] for i in mine], axis=1) for part in range(2)], axis=0
        )
        term = dot(left, jnp.concatenate([cell_v[i] for i in mine], axis=0))
        total = term if total is None else total + term
    block = (total[:rank] + turn(total[rank:])).astype(BF16)
    out[...] = block
    joint[:rank, :] = block
    for c in copies[4:]:
        c.wait()


def fetch_table(table_v, table, sem):
    copy = pltpu.make_async_copy(table_v, table, sem.at[0])
    copy.start()
    return copy


def local_kernel(
    table_v, source, solve, down_ref, parent_ref, _, local, maps, table, table_sem, *, groups
):
    fetched = fetch_table(table_v, table, table_sem)
    cells, nodes, width = source.shape
    position = lax.axis_index("loop")
    for g, group in enumerate(groups[:-1]):
        if len(group) == 2:
            low, high = group
            re, im = rows_of(parent_ref, low, (position >> low) & 1)
            inner = jnp.concatenate(rows_of(down_ref, high, (position >> high) & 1), axis=0)
            maps[g] = jnp.concatenate(split(side_by_side(times(re, im, inner))), axis=0)
    slots = slot_count(cells, solve.shape[0])
    fetched.wait()
    pairs = Pairs(table, slots)
    for s in range(slots):
        k, a, b = pairs[s]
        va, vb = source[a], source[b]
        right = jnp.concatenate(
            [
                jnp.concatenate([va, vb], axis=1),
                jnp.concatenate([turned(va), turned(vb)], axis=1),
            ],
            axis=0,
        )
        value = dot(wide(solve, k), right)
        local[a] = value[:, :width]
        local[b] = value[:, width:]


def gather_nodes(group, position, own, arrived, nodes_v):
    count = 1 << len(group)
    index = (position >> group[0]) & (count - 1)
    rank = own.shape[0]
    for mask in range(count):
        value = own[...] if mask == 0 else arrived[mask - 1][:rank, :]
        where = index ^ mask
        nodes_v[where] = value
        nodes_v[count + where] = turned(value)


def pair_stack(nodes_v, count, first):
    return jnp.concatenate(
        [nodes_v[first], nodes_v[first + 1], nodes_v[count + first], nodes_v[count + first + 1]],
        axis=0,
    )


def middle_stack(group, nodes_v, up_ref):
    both = jnp.concatenate([pair_stack(nodes_v, 4, 0), pair_stack(nodes_v, 4, 2)], axis=1)
    y = dot(wide(up_ref, group[0]), both)
    width = y.shape[1] // 2
    parts = [y[:, :width], y[:, width:]]
    return split(jnp.concatenate(parts + [turn(p) for p in parts], axis=0))


def combine_kernel(maps, up_ref, down_ref, own, *refs, group, index):
    count = 1 << len(group)
    arrived = refs[: count - 1]
    node, part, nodes_v = refs[count - 1 :]
    position = lax.axis_index("loop")
    gather_nodes(group, position, own, arrived, nodes_v)
    low_down = jnp.concatenate(rows_of(down_ref, group[0], (position >> group[0]) & 1), axis=1)
    if len(group) == 1:
        stack = pair_stack(nodes_v, 2, 0)
        node[...] = dot(wide(up_ref, group[0]), stack).astype(BF16)
        part[...] = dot(low_down, stack)
        return
    high, low = middle_stack(group, nodes_v, up_ref)
    rank = own.shape[0]
    up = wide(up_ref, group[1])
    node[...] = (dot(up, high) + dot(up, low)).astype(BF16)
    mine = pair_stack(nodes_v, 4, 2 * ((position >> group[1]) & 1))
    map_high, map_low = maps[index, :rank], maps[index, rank:]
    part[...] = (
        dot(map_high, high) + dot(map_high, low) + dot(map_low, high) + dot(low_down, mine)
    )


def perturb_kernel(
    table_v,
    forward,
    joint,
    odd,
    rim_left,
    rim_right,
    shape_ref,
    angle_ref,
    weight_ref,
    ids_ref,
    up_ref,
    down_ref,
    parent_ref,
    root_ref,
    _,
    weighted,
    final_map,
    columns,
    table,
    table_sem,
    *,
    groups,
    device_count,
):
    fetched = fetch_table(table_v, table, table_sem)
    cells, nodes, width = forward.shape
    rim = odd.shape[0]
    classes = shape_ref.shape[0]
    position = lax.axis_index("loop")
    parity = position & 1

    group = groups[-1]
    top = group[-1]
    total = times(root_ref[0], root_ref[1], tall(up_ref, top))
    for level in reversed(group):
        bit = (position >> level) & 1
        re, im = rows_of(parent_ref, level, bit)
        total = times(re, im, total)
        down = jnp.concatenate(rows_of(down_ref, level, bit), axis=0).astype(F32)
        if level == top:
            total = total + down
        else:
            total = jnp.concatenate([total, down], axis=1)
    for lower in reversed(groups[:-1]):
        for level in reversed(lower):
            re, im = rows_of(parent_ref, level, (position >> level) & 1)
            total = times(re, im, total)
    pieces = [total[:, c : c + down.shape[1]] for c in range(0, total.shape[1], down.shape[1])]
    whole = jnp.concatenate([side_by_side(p) for p in pieces], axis=1)
    final_map[...] = jnp.concatenate(split(whole), axis=0)

    ids = jnp.concatenate([ids_ref[...], ids_ref[...]], axis=1)
    entries = angle_ref.shape[1]
    chosen = lax.broadcasted_iota(jnp.int32, (entries, width), 0) == ids

    def looked_up(row):
        column = jnp.transpose(jnp.broadcast_to(row, (8, entries)))[:, :1]
        return jnp.sum(jnp.where(chosen, column, 0.0), axis=0, keepdims=True)

    scale = half_sign(width) * (-1.0 / math.sqrt(nodes * (width // 2)))
    weights = looked_up(weight_ref[...]) * scale
    for k in range(classes):
        flipped = jnp.transpose(jnp.concatenate([shape_ref[k]] * 4, axis=0))
        columns[k, 0] = jnp.broadcast_to(flipped[:, 0:1], (nodes, width)) * weights
        columns[k, 1] = jnp.broadcast_to(flipped[:, 1:2], (nodes, width)) * weights

    even = joint[joint.shape[0] - rim :, :]
    before = jnp.where(parity == 1, even, odd[...])
    after = jnp.where(parity == 0, even, odd[...])

    def left_input(p):
        return jnp.where(p == 0, before, forward[jnp.maximum(p - 1, 0), nodes - rim :, :])

    def right_input(p):
        return jnp.where(p == cells - 1, after, forward[jnp.minimum(p + 1, cells - 1), :rim, :])

    def stacked(values):
        return jnp.concatenate(
            [
                jnp.concatenate(values, axis=1),
                jnp.concatenate([turned(v) for v in values], axis=1),
            ],
            axis=0,
        )

    slots = slot_count(cells, classes)
    pairs = Pairs(table, slots)
    fetched.wait()
    for s in range(slots):
        k, a, b = pairs[s]
        left = dot(wide(rim_left, k), stacked([left_input(a), left_input(b)]))
        right = dot(wide(rim_right, k), stacked([right_input(a), right_input(b)]))
        for i, p in enumerate((a, b)):
            field = forward[p].astype(F32)
            value = columns[k, 0] * field + columns[k, 1] * turn(field)
            lanes = slice(i * width, (i + 1) * width)
            weighted[p, :rim, :] = value[:rim] + left[:, lanes] * weights
            weighted[p, rim : nodes - rim, :] = value[rim : nodes - rim]
            weighted[p, nodes - rim :, :] = value[nodes - rim :] + right[:, lanes] * weights

    def seam(ref, k, block, sign):
        angles = looked_up(angle_ref[...])
        term = dot(wide(ref, k), jnp.concatenate([block, turned(block)], axis=0))
        turned_term = term * jnp.cos(angles) + turn(term) * (jnp.sin(angles) * sign)
        return (turned_term - term) * weights

    ends = pairs.ends()

    @pl.when(position == 0)
    def _first():
        weighted[0, :rim, :] += seam(rim_left, ends[0], before, -1.0)

    @pl.when(position == device_count - 1)
    def _last():
        weighted[cells - 1, nodes - rim :, :] += seam(rim_right, ends[1], after, 1.0)


def down_kernel(table_v, final_map, up_ref, own, *refs, group):
    count = 1 << len(group)
    arrived = refs[: count - 1]
    part, split_ref, lift, local, weighted, adjoint, gradient = refs[count - 1 : count + 6]
    nodes_v, cell_v, out_v, sums, sems, table, table_sem = refs[count + 6 :]
    fetched = fetch_table(table_v, table, table_sem)
    rank = own.shape[0]
    cells, nodes, width = local.shape
    position = lax.axis_index("loop")
    gather_nodes(group, position, own, arrived, nodes_v)
    map_high, map_low = final_map[:rank], final_map[rank:]
    if len(group) == 1:
        stack = pair_stack(nodes_v, 2, 0)
        field = dot(map_high, stack) + dot(map_low, stack)
    else:
        high, low = middle_stack(group, nodes_v, up_ref)
        mine = pair_stack(nodes_v, 4, 2 * ((position >> group[1]) & 1))
        stack = jnp.concatenate([high, mine], axis=0)
        field = dot(map_high, stack) + dot(map_low, stack) + dot(map_high[:, : low.shape[0]], low)
    field = field + part[...]
    both = jnp.concatenate([field.astype(BF16), turn(field).astype(BF16)], axis=0)
    for p in range(cells):
        cell = dot(wide(split_ref, p), both)
        cell_v[p] = jnp.concatenate([cell.astype(BF16), turn(cell).astype(BF16)], axis=0)

    slots = slot_count(cells, lift.shape[0])
    pairs = Pairs(table, slots)
    fetched.wait()

    def send(p):
        return pltpu.make_async_copy(out_v.at[p], adjoint.at[p], sems.at[p])

    def lift_pair(s):
        k, a, b = pairs[s]
        value = dot(wide(lift, k), jnp.concatenate([cell_v[a], cell_v[b]], axis=1))
        for i, p in enumerate((a, b)):
            rounded = (local[p] + value[:, i * width : (i + 1) * width]).astype(BF16)
            out_v[p] = rounded
            total = jnp.sum(rounded.astype(F32) * weighted[p], axis=0, keepdims=True)
            sums[p] = jnp.broadcast_to(total, (8, width))
        send(a).start()

        @pl.when(a != b)
        def _():
            send(b).start()

    for s in range(slots):
        if s < (cells + 1) // 2:
            lift_pair(s)
        else:
            pl.when(s < pairs.used())(functools.partial(lift_pair, s))

    rows = jnp.concatenate([sums[p, :1] for p in range(cells)], axis=0)
    row = lax.broadcasted_iota(jnp.int32, (cells, cells), 0)
    lane = lax.broadcasted_iota(jnp.int32, (cells, cells), 1)
    across = jnp.sum(rows, axis=1, keepdims=True)
    gradient[...] = jnp.sum(jnp.where(row == lane, across, 0.0), axis=0, keepdims=True)
    for p in range(cells):
        send(p).wait()


def shards(
    classes,
    forward_field,
    adjoint_source,
    leaf_solve,
    leaf_lift,
    leaf_skeleton,
    block_merge,
    block_split,
    level_up,
    level_down,
    level_parent,
    root_solve,
    rim_left,
    rim_right,
    shape_derivative,
    illum_angle,
    illum_weight,
    illum_ids,
):
    position = lax.axis_index("loop")
    device_count = lax.axis_size("loop")
    cells, nodes, width = adjoint_source.shape
    class_count = leaf_solve.shape[0]
    rank = root_solve.shape[-1]
    rim = rim_left.shape[-1]
    levels = level_up.shape[0]
    groups = groups_of(levels)
    slots = slot_count(cells, class_count)
    sds = jax.ShapeDtypeStruct
    node = sds((rank, width), BF16)
    halo = sds((rim, width), BF16)

    size = table_size(slots)
    table_scratch = [pltpu.SMEM((size,), jnp.int32), pltpu.SemaphoreType.DMA((1,))]
    pinned = functools.partial(pltpu.with_memory_space_constraint, memory_space=pltpu.HBM)
    source, joint, odd, table = pl.pallas_call(
        up_kernel,
        out_shape=(node, sds((rank + rim, width), BF16), halo, sds((size,), jnp.int32)),
        in_specs=[HBM] * 5,
        out_specs=(VM, VM, VM, VM),
        scratch_shapes=[
            pltpu.SMEM((cells,), jnp.int32),
            pltpu.SMEM((size,), jnp.int32),
            pltpu.VMEM((cells, nodes, width), BF16),
            pltpu.VMEM((class_count, 2, rank, nodes), BF16),
            pltpu.VMEM(block_merge.shape, BF16),
            pltpu.VMEM((cells, rank, width), BF16),
            pltpu.SemaphoreType.DMA((7,)),
        ],
        compiler_params=params(8),
        cost_estimate=cost(64 * cells * rank * nodes * width, 64 * MIB),
        name="up",
    )(*map(pinned, (classes, adjoint_source, leaf_skeleton, block_merge, forward_field)))

    def exchange(value, mask):
        pairs = [(i, i ^ mask) for i in range(device_count)]
        return lax.ppermute(value, "loop", pairs)

    def odd_exchange(value):
        pairs = [
            (i, (i + 1) % device_count if i % 2 else (i - 1) % device_count)
            for i in range(device_count)
        ]
        return lax.ppermute(value, "loop", pairs)

    def gather(value, group):
        base = 1 << group[0]
        return [exchange(value, base * m) for m in range(1, 1 << len(group))]

    odd_in = odd_exchange(odd)
    arrived = [exchange(joint, 1)] + [
        exchange(source, m) for m in range(2, 1 << len(groups[0]))
    ]
    joint_in = arrived[0]

    local, maps = pl.pallas_call(
        functools.partial(local_kernel, groups=groups),
        out_shape=(
            sds((cells, nodes, width), F32),
            sds((max(len(groups) - 1, 1), 2 * rank, 4 * rank), BF16),
        ),
        in_specs=[VM] * 6,
        out_specs=(VM, VM),
        scratch_shapes=table_scratch,
        compiler_params=params(4),
        cost_estimate=cost(8 * cells * nodes * nodes * width, 6 * MIB),
        name="local",
    )(table, adjoint_source, leaf_solve, level_down, level_parent, source)

    own = source
    fields = []
    for g, group in enumerate(groups[:-1]):
        count = 1 << len(group)
        own, part = pl.pallas_call(
            functools.partial(combine_kernel, group=group, index=g),
            out_shape=(node, sds((rank, width), F32)),
            in_specs=[VM] * (3 + count),
            out_specs=(VM, VM),
            scratch_shapes=[pltpu.VMEM((2 * count, rank, width), BF16)],
            compiler_params=params(4),
            cost_estimate=cost(16 * rank * rank * width, MIB),
            name="combine",
        )(maps, level_up, level_down, own, *arrived)
        fields.append((group, part))
        arrived = gather(own, groups[g + 1])

    group = groups[-1]
    count = 1 << len(group)
    weighted, final_map = pl.pallas_call(
        functools.partial(perturb_kernel, groups=groups, device_count=device_count),
        out_shape=(
            sds((cells, nodes, width), F32),
            sds((2 * rank, 2 * (rank << len(group))), BF16),
        ),
        in_specs=[VM] * 15,
        out_specs=(VM, VM),
        scratch_shapes=[pltpu.VMEM((class_count, 2, nodes, width), F32)] + table_scratch,
        compiler_params=params(8),
        cost_estimate=cost(8 * cells * rim * rim * width, 4 * MIB),
        name="perturb",
    )(
        table,
        forward_field,
        joint_in,
        odd_in,
        rim_left,
        rim_right,
        shape_derivative,
        illum_angle[None],
        illum_weight[None],
        illum_ids[None],
        level_up,
        level_down,
        level_parent,
        root_solve,
        own,
    )

    part = fold_parts(fields, level_parent, position, rank, width)
    adjoint, gradient = pl.pallas_call(
        functools.partial(down_kernel, group=group),
        out_shape=(sds((cells, nodes, width), BF16), sds((1, cells), F32)),
        in_specs=[VM] * (count + 3 + 5),
        out_specs=(HBM, VM),
        scratch_shapes=[
            pltpu.VMEM((2 * count, rank, width), BF16),
            pltpu.VMEM((cells, 2 * rank, width), BF16),
            pltpu.VMEM((cells, nodes, width), BF16),
            pltpu.VMEM((cells, 8, width), F32),
            pltpu.SemaphoreType.DMA((cells,)),
        ]
        + table_scratch,
        compiler_params=params(6),
        cost_estimate=cost(8 * cells * nodes * rank * width, 8 * MIB),
        name="down",
    )(table, final_map, level_up, own, *arrived, part, block_split, leaf_lift, local, weighted)
    return adjoint, gradient[0]


def fold_parts(fields, level_parent, position, rank, width):
    if not fields:
        return jnp.zeros((rank, width), F32)
    total = fields[-1][1]
    for group, part in reversed(fields[:-1]):
        for level in reversed(group):
            start = ((position >> level) & 1) * rank
            rows = lax.dynamic_slice_in_dim(level_parent[level], start, rank, 1).astype(F32)
            direct = jnp.dot(rows[0], total, precision=lax.Precision.HIGHEST)
            twisted = jnp.dot(rows[1], total, precision=lax.Precision.HIGHEST)
            half = width // 2
            total = direct + jnp.concatenate([-twisted[:, half:], twisted[:, :half]], axis=1)
        total = total + part
    return total


def solution(mesh):
    return jax.shard_map(
        shards,
        mesh=mesh,
        in_specs=(
            P(("parts", "loop")),
            P(("parts", "loop"), None, None),
            P(("parts", "loop"), None, None),
            P("parts", None, None, None),
            P("parts", None, None, None),
            P("parts", None, None, None),
            P("parts", None, None, None),
            P("parts", None, None, None),
            P("parts", None, None, None),
            P("parts", None, None, None),
            P("parts", None, None, None),
            P("parts", None, None),
            P("parts", None, None, None),
            P("parts", None, None, None),
            P("parts", None, None),
            P("parts"),
            P("parts"),
            P(),
        ),
        out_specs=(P(("parts", "loop"), None, None), P(("parts", "loop"))),
        check_vma=False,
    )
```

```python
import functools
import math

import jax
import jax.numpy as jnp
from jax import lax
from jax.experimental import pallas as pl
from jax.experimental.pallas import tpu as pltpu
from jax.sharding import PartitionSpec as P

F32 = jnp.float32
BF16 = jnp.bfloat16
MIB = 1 << 20
VM = pl.BlockSpec(memory_space=pltpu.VMEM)
HBM = pl.BlockSpec(memory_space=pltpu.HBM)


def params(mib):
    return pltpu.CompilerParams(vmem_limit_bytes=mib * MIB)


def cost(flops, nbytes):
    return pl.CostEstimate(flops=flops, bytes_accessed=nbytes, transcendentals=0)


def half_sign(width):
    lane = lax.broadcasted_iota(jnp.int32, (1, width), 1)
    return jnp.where(lane < width // 2, -1.0, 1.0).astype(F32)


def turn(values):
    width = values.shape[-1]
    return pltpu.roll(values, width // 2, 1) * half_sign(width)


def dot(a, b):
    return jnp.dot(a, b, preferred_element_type=F32)


def split(x):
    high = x.astype(BF16)
    return high, (x - high.astype(F32)).astype(BF16)


def embed(re, im):
    return jnp.concatenate(
        [jnp.concatenate([re, -im], axis=1), jnp.concatenate([im, re], axis=1)], axis=0
    )


def times(re, im, stacked):
    left = embed(re, im)
    if stacked.dtype == BF16:
        return dot(left, stacked)
    high, low = split(stacked)
    return dot(left, high) + dot(left, low)


def side_by_side(stacked):
    rows = stacked.shape[0] // 2
    return jnp.concatenate([stacked[:rows], stacked[rows:]], axis=1)


def wide(ref, *at):
    return jnp.concatenate([ref[(*at, 0)], ref[(*at, 1)]], axis=1)


def tall(ref, *at):
    return jnp.concatenate([ref[(*at, 0)], ref[(*at, 1)]], axis=0)


def rows_of(ref, level, bit):
    rank = ref.shape[2] // 2
    start = pl.multiple_of(bit * rank, rank)
    return ref[level, 0, pl.ds(start, rank), :], ref[level, 1, pl.ds(start, rank), :]


def turned(value):
    return turn(value.astype(F32)).astype(BF16)


def slot_count(cells, classes):
    return (cells + classes) // 2


def table_size(slots):
    return -(-(3 * slots + 3) // 128) * 128


class Pairs:
    def __init__(self, table, slots):
        self.table, self.slots = table, slots

    def ends(self):
        return self.table[3 * self.slots + 1], self.table[3 * self.slots + 2]

    def __getitem__(self, slot):
        return tuple(self.table[i * self.slots + slot] for i in range(3))

    def used(self):
        return self.table[3 * self.slots]


def fill_pairs(scal, table, cells, classes):
    slots = slot_count(cells, classes)
    slot = jnp.int32(0)
    for k in range(classes):
        half = jnp.int32(0)
        for p in range(cells):
            mine = scal[p] == k

            @pl.when(jnp.logical_and(mine, half == 0))
            def _first(k=k, p=p, slot=slot):
                table[slot] = k
                table[slots + slot] = p

            @pl.when(mine)
            def _second(p=p, slot=slot):
                table[2 * slots + slot] = p

            step = mine.astype(jnp.int32)
            slot = slot + step * half
            half = jnp.where(mine, 1 - half, half)
        slot = slot + half
    table[3 * slots] = slot
    table[3 * slots + 1] = scal[0]
    table[3 * slots + 2] = scal[cells - 1]
    for s in range((cells + 1) // 2, slots):

        @pl.when(s >= slot)
        def _spare(s=s):
            for i in range(3):
                table[i * slots + s] = table[i * slots]


def up_kernel(
    classes_h,
    source,
    skeleton,
    merge,
    forward,
    joint,
    table_out,
    src_v,
    scal,
    table,
    skel_v,
    merge_v,
    cell_v,
    sems,
):
    cells, nodes, width = src_v.shape
    classes = skel_v.shape[0]
    rank = skel_v.shape[2]
    rim = (joint.shape[0] - rank) // 2
    parity = lax.axis_index("loop") & 1
    copies = []

    def start(src, dst, i):
        c = pltpu.make_async_copy(src, dst, sems.at[i])
        c.start()
        copies.append(c)

    start(classes_h, scal, 0)
    start(skeleton, skel_v, 1)
    start(source, src_v, 2)
    start(merge, merge_v, 3)
    last = (cells - 1, nodes - rim)
    even_cell = jnp.where(parity == 0, last[0], 0)
    even_row = pl.multiple_of(jnp.where(parity == 0, last[1], 0), rim)
    odd_cell = jnp.where(parity == 1, last[0], 0)
    odd_row = pl.multiple_of(jnp.where(parity == 1, last[1], 0), rim)
    start(forward.at[even_cell, pl.ds(even_row, rim), :], joint.at[pl.ds(rank, rim), :], 4)
    start(forward.at[odd_cell, pl.ds(odd_row, rim), :], joint.at[pl.ds(rank + rim, rim), :], 5)
    copies[0].wait()
    fill_pairs(scal, table, cells, classes)
    start(table, table_out, 6)
    slots = slot_count(cells, classes)
    pairs = Pairs(table, slots)
    copies[1].wait()
    copies[2].wait()
    for s in range(slots):
        k, a, b = pairs[s]
        both = dot(tall(skel_v, k), jnp.concatenate([src_v[a], src_v[b]], axis=1))
        for i, p in enumerate((a, b)):
            part = both[:, i * width : (i + 1) * width]
            for j, piece in enumerate(split(part[:rank] + turn(part[rank:]))):
                cell_v[j, p] = piece
    copies[3].wait()
    total = None
    for p in range(0, cells, 2):
        mine = range(p, min(p + 2, cells))
        left = jnp.concatenate(
            [jnp.concatenate([merge_v[i, part] for i in mine], axis=1) for part in range(2)], axis=0
        )
        for j in range(2):
            term = dot(left, jnp.concatenate([cell_v[j, i] for i in mine], axis=0))
            total = term if total is None else total + term
    joint[:rank, :] = (total[:rank] + turn(total[rank:])).astype(BF16)
    for c in copies[4:]:
        c.wait()


def fetch_table(table_v, table, sem):
    copy = pltpu.make_async_copy(table_v, table, sem.at[0])
    copy.start()
    return copy


def maps_kernel(up_ref, down_ref, parent_ref, root_ref, _, maps):
    levels = up_ref.shape[0]
    position = lax.axis_index("loop")

    def bit(level):
        return (position >> level) & 1

    for level in range(1, levels):
        total = jnp.concatenate(rows_of(down_ref, level, bit(level)), axis=0)
        if level == levels - 1:
            above = times(root_ref[0], root_ref[1], tall(up_ref, level))
            re, im = rows_of(parent_ref, level, bit(level))
            total = total.astype(F32) + times(re, im, above)
        for lower in reversed(range(level)):
            re, im = rows_of(parent_ref, lower, bit(lower))
            total = times(re, im, total)
        maps[level - 1] = jnp.concatenate(split(side_by_side(total)), axis=0)


def local_kernel(table_v, source, solve, _, local, table, table_sem):
    fetched = fetch_table(table_v, table, table_sem)
    cells, nodes, width = source.shape
    slots = slot_count(cells, solve.shape[0])
    fetched.wait()
    pairs = Pairs(table, slots)
    for s in range(slots):
        k, a, b = pairs[s]
        va, vb = source[a], source[b]
        right = jnp.concatenate(
            [
                jnp.concatenate([va, vb], axis=1),
                jnp.concatenate([turned(va), turned(vb)], axis=1),
            ],
            axis=0,
        )
        value = dot(wide(solve, k), right)
        local[a] = value[:, :width]
        local[b] = value[:, width:]


def sibling_stack(level, own, arrived, nodes_v):
    rank, width = nodes_v.shape[1:]
    mine = (lax.axis_index("loop") >> level) & 1
    for ref, where in ((own, mine), (arrived, 1 - mine)):
        value = ref[:rank, :]
        nodes_v[where] = value
        nodes_v[2 + where] = turned(value)
    return nodes_v[...].reshape(4 * rank, width)


def combine_kernel(maps, up_ref, own, arrived, *refs, level):
    (joint, part, nodes_v), before = refs[-3:], refs[:-3]
    rank = nodes_v.shape[1]
    rim = joint.shape[0] - rank
    joint[rank:, :] = arrived[arrived.shape[0] - rim :, :]
    stack = sibling_stack(level, own, arrived, nodes_v)
    joint[:rank, :] = dot(wide(up_ref, level), stack).astype(BF16)
    if level == 0:
        bit = lax.axis_index("loop") & 1
        part[...] = dot(jnp.concatenate(rows_of(maps, 0, bit), axis=1), stack)
    else:
        both = dot(maps[level - 1], stack)
        part[...] = before[0][...] + both[:rank] + both[rank:]


def rows_kernel(
    classes_ref, rim_left, rim_right, shape_ref, angle_ref, weight_ref, ids_ref, _, columns, edge_map, rows_out, scal, sem, *, device_count
):
    fetched = fetch_table(classes_ref, scal, sem)
    classes, _, nodes, width = columns.shape
    position = lax.axis_index("loop")
    ids = jnp.concatenate([ids_ref[...], ids_ref[...]], axis=1)
    entries = angle_ref.shape[1]
    chosen = lax.broadcasted_iota(jnp.int32, (entries, width), 0) == ids

    def looked_up(row):
        column = jnp.transpose(jnp.broadcast_to(row, (8, entries)))[:, :1]
        return jnp.sum(jnp.where(chosen, column, 0.0), axis=0, keepdims=True)

    scale = half_sign(width) * (-1.0 / math.sqrt(nodes * (width // 2)))
    weights = looked_up(weight_ref[...]) * scale
    angles = looked_up(angle_ref[...])
    at_start, at_end = position == 0, position == device_count - 1
    cosine = jnp.where(jnp.logical_or(at_start, at_end), jnp.cos(angles), 1.0)
    sine = jnp.sin(angles)
    sine = jnp.where(at_start, -sine, jnp.where(at_end, sine, 0.0))
    for i, row in enumerate((weights, cosine, sine)):
        rows_out[i] = jnp.broadcast_to(row, (8, width))
    for k in range(classes):
        flipped = jnp.transpose(jnp.concatenate([shape_ref[k]] * 4, axis=0))
        columns[k, 0] = jnp.broadcast_to(flipped[:, 0:1], (nodes, width)) * weights
        columns[k, 1] = jnp.broadcast_to(flipped[:, 1:2], (nodes, width)) * weights

    cells = scal.shape[0]
    fetched.wait()
    first, last = scal[0], scal[cells - 1]

    @pl.when((position & 1) == 0)
    def _left():
        edge_map[...] = wide(rim_left, first)

    @pl.when((position & 1) == 1)
    def _right():
        edge_map[...] = wide(rim_right, last)


def perturb_kernel(table_v, forward, joint_in, rim_left, rim_right, columns, rows, _, weighted, table, table_sem):
    fetched = fetch_table(table_v, table, table_sem)
    cells, nodes, width = forward.shape
    rim = rim_left.shape[-1]
    rank = joint_in.shape[0] - 2 * rim
    classes = rim_left.shape[0]
    parity = lax.axis_index("loop") & 1
    weights = rows[0, :1]
    even = joint_in[rank : rank + rim, :]
    none = jnp.zeros_like(even)
    before = jnp.where(parity == 1, even, none)
    after = jnp.where(parity == 0, even, none)

    def left_input(p):
        return jnp.where(p == 0, before, forward[jnp.maximum(p - 1, 0), nodes - rim :, :])

    def right_input(p):
        return jnp.where(p == cells - 1, after, forward[jnp.minimum(p + 1, cells - 1), :rim, :])

    def stacked(values):
        return jnp.concatenate(
            [
                jnp.concatenate(values, axis=1),
                jnp.concatenate([turned(v) for v in values], axis=1),
            ],
            axis=0,
        )

    slots = slot_count(cells, classes)
    pairs = Pairs(table, slots)
    fetched.wait()
    for s in range(slots):
        k, a, b = pairs[s]
        left = dot(wide(rim_left, k), stacked([left_input(a), left_input(b)]))
        right = dot(wide(rim_right, k), stacked([right_input(a), right_input(b)]))
        for i, p in enumerate((a, b)):
            field = forward[p].astype(F32)
            value = columns[k, 0] * field + columns[k, 1] * turn(field)
            lanes = slice(i * width, (i + 1) * width)
            weighted[p, :rim, :] = value[:rim] + left[:, lanes] * weights
            weighted[p, rim : nodes - rim, :] = value[rim : nodes - rim]
            weighted[p, nodes - rim :, :] = value[nodes - rim :] + right[:, lanes] * weights


def odd_block(edges, position, rim):
    value = None
    for level in reversed(range(1, len(edges) + 1)):
        ref = edges[level - 1]
        rows = ref[ref.shape[0] - rim :, :]
        here = ((position >> level) & 1) != (position & 1)
        value = rows if value is None else jnp.where(here, rows, value)
    return value


def down_kernel(table_v, maps, edge_map, rows_ref, own, arrived, *refs, level):
    edges, refs = refs[: level - 1] + (arrived,), refs[level - 1 :]
    part, split_ref, lift, local, weighted, adjoint, gradient = refs[:7]
    nodes_v, cell_v, out_v, sums, sems, table, table_sem = refs[7:]
    fetched = fetch_table(table_v, table, table_sem)
    rank = nodes_v.shape[1]
    cells, nodes, width = local.shape
    position = lax.axis_index("loop")
    rim = edge_map.shape[0]
    block = odd_block(edges, position, rim)
    edge = dot(edge_map[...], jnp.concatenate([block, turned(block)], axis=0))
    edge = (edge * rows_ref[1, :1] + turn(edge) * rows_ref[2, :1]) * rows_ref[0, :1]
    stack = sibling_stack(level, own, arrived, nodes_v)
    halves = dot(maps[level - 1], stack)
    field = halves[:rank] + halves[rank:] + part[...]
    both, rest = split(jnp.concatenate([field, turn(field)], axis=0))
    for p in range(cells):
        cell = dot(wide(split_ref, p), both) + dot(wide(split_ref, p), rest)
        cell_v[p] = jnp.concatenate([cell.astype(BF16), turn(cell).astype(BF16)], axis=0)

    slots = slot_count(cells, lift.shape[0])
    pairs = Pairs(table, slots)
    fetched.wait()

    def send(p):
        return pltpu.make_async_copy(out_v.at[p], adjoint.at[p], sems.at[p])

    def lift_pair(s):
        k, a, b = pairs[s]
        value = dot(wide(lift, k), jnp.concatenate([cell_v[a], cell_v[b]], axis=1))
        for i, p in enumerate((a, b)):
            rounded = (local[p] + value[:, i * width : (i + 1) * width]).astype(BF16)
            out_v[p] = rounded
            total = jnp.sum(rounded.astype(F32) * weighted[p], axis=0, keepdims=True)
            sums[p] = jnp.broadcast_to(total, (8, width))
        send(a).start()

        @pl.when(a != b)
        def _():
            send(b).start()

    for s in range(slots):
        if s < (cells + 1) // 2:
            lift_pair(s)
        else:
            pl.when(s < pairs.used())(functools.partial(lift_pair, s))

    parity = position & 1
    edge_cell = jnp.where(parity == 0, 0, cells - 1)
    edge_row = pl.multiple_of(jnp.where(parity == 0, 0, nodes - rim), rim)
    outer = out_v[edge_cell, pl.ds(edge_row, rim), :].astype(F32)
    sums[edge_cell] += jnp.broadcast_to(jnp.sum(outer * edge, axis=0, keepdims=True), (8, width))
    rows = jnp.concatenate([sums[p, :1] for p in range(cells)], axis=0)
    row = lax.broadcasted_iota(jnp.int32, (cells, cells), 0)
    lane = lax.broadcasted_iota(jnp.int32, (cells, cells), 1)
    across = jnp.sum(rows, axis=1, keepdims=True)
    gradient[...] = jnp.sum(jnp.where(row == lane, across, 0.0), axis=0, keepdims=True)
    for p in range(cells):
        send(p).wait()


def shards(
    classes,
    forward_field,
    adjoint_source,
    leaf_solve,
    leaf_lift,
    leaf_skeleton,
    block_merge,
    block_split,
    level_up,
    level_down,
    level_parent,
    root_solve,
    rim_left,
    rim_right,
    shape_derivative,
    illum_angle,
    illum_weight,
    illum_ids,
):
    position = lax.axis_index("loop")
    device_count = lax.axis_size("loop")
    cells, nodes, width = adjoint_source.shape
    class_count = leaf_solve.shape[0]
    rank = root_solve.shape[-1]
    rim = rim_left.shape[-1]
    levels = level_up.shape[0]
    slots = slot_count(cells, class_count)
    sds = jax.ShapeDtypeStruct
    joint = sds((rank + rim, width), BF16)
    size = table_size(slots)
    table_scratch = [pltpu.SMEM((size,), jnp.int32), pltpu.SemaphoreType.DMA((1,))]
    pinned = functools.partial(pltpu.with_memory_space_constraint, memory_space=pltpu.HBM)
    node, table, source_v = pl.pallas_call(
        up_kernel,
        out_shape=(
            sds((rank + 2 * rim, width), BF16),
            sds((size,), jnp.int32),
            sds((cells, nodes, width), BF16),
        ),
        in_specs=[HBM] * 5,
        out_specs=(VM,) * 3,
        scratch_shapes=[
            pltpu.SMEM((cells,), jnp.int32),
            pltpu.SMEM((size,), jnp.int32),
            pltpu.VMEM((class_count, 2, rank, nodes), BF16),
            pltpu.VMEM(block_merge.shape, BF16),
            pltpu.VMEM((2, cells, rank, width), BF16),
            pltpu.SemaphoreType.DMA((7,)),
        ],
        compiler_params=params(8),
        cost_estimate=cost(64 * cells * rank * nodes * width, 64 * MIB),
        name="up",
    )(*map(pinned, (classes, adjoint_source, leaf_skeleton, block_merge, forward_field)))

    def exchange(value, level):
        pairs = [(i, i ^ (1 << level)) for i in range(device_count)]
        return lax.ppermute(value, "loop", pairs)

    def make_maps(after):
        return pl.pallas_call(
            maps_kernel,
            out_shape=sds((max(levels - 1, 1), 2 * rank, 4 * rank), BF16),
            in_specs=[VM] * 5,
            out_specs=VM,
            compiler_params=params(4),
            cost_estimate=cost(1 << 30, 4 * MIB),
            name="maps",
        )(level_up, level_down, level_parent, root_solve, after)

    def make_local(after):
        return pl.pallas_call(
            local_kernel,
            out_shape=sds((cells, nodes, width), F32),
            in_specs=[VM] * 4,
            out_specs=VM,
            scratch_shapes=table_scratch,
            compiler_params=params(4),
            cost_estimate=cost(8 * cells * nodes * nodes * width, 6 * MIB),
            name="local",
        )(table, source_v, leaf_solve, after)

    def make_rows(after):
        return pl.pallas_call(
            functools.partial(rows_kernel, device_count=device_count),
            out_shape=(
                sds((class_count, 2, nodes, width), F32),
                sds((rim, 2 * rim), BF16),
                sds((3, 8, width), F32),
            ),
            in_specs=[VM] * 8,
            out_specs=(VM,) * 3,
            scratch_shapes=[pltpu.SMEM((cells,), jnp.int32), pltpu.SemaphoreType.DMA((1,))],
            compiler_params=params(4),
            cost_estimate=cost(1 << 30, 4 * MIB),
            name="rows",
        )(
            classes,
            rim_left,
            rim_right,
            shape_derivative,
            illum_angle[None],
            illum_weight[None],
            illum_ids[None],
            after,
        )

    def make_weighted(after):
        return pl.pallas_call(
            perturb_kernel,
            out_shape=sds((cells, nodes, width), F32),
            in_specs=[VM] * 8,
            out_specs=VM,
            scratch_shapes=table_scratch,
            compiler_params=params(4),
            cost_estimate=cost(1 << 30, 4 * MIB),
            name="perturb",
        )(table, forward_field, even_in, rim_left, rim_right, columns, rows, after)

    arrived = even_in = exchange(node, 0)
    edges = []
    part = ()
    maps = make_maps(node)
    for level in range(levels - 1):
        node, *part = pl.pallas_call(
            functools.partial(combine_kernel, level=level),
            out_shape=(joint, sds((rank, width), F32)),
            in_specs=[VM] * (4 + len(part)),
            out_specs=(VM, VM),
            scratch_shapes=[pltpu.VMEM((4, rank, width), BF16)],
            compiler_params=params(4),
            cost_estimate=cost(16 * rank * rank * width, MIB),
            name="combine",
        )(maps if level else level_down, level_up, node, arrived, *part)
        arrived = exchange(node, level + 1)
        edges.append(arrived)
        last = level == levels - 2
        if level == 0:
            local = make_local(node)
        if level == 1 or (last and level < 1):
            columns, edge_map, rows = make_rows(node)
        if level == 2 or (last and level < 2):
            weighted = make_weighted(node)

    adjoint, gradient = pl.pallas_call(
        functools.partial(down_kernel, level=levels - 1),
        out_shape=(sds((cells, nodes, width), BF16), sds((1, cells), F32)),
        in_specs=[VM] * (6 + len(edges) - 1 + 5),
        out_specs=(HBM, VM),
        scratch_shapes=[
            pltpu.VMEM((4, rank, width), BF16),
            pltpu.VMEM((cells, 2 * rank, width), BF16),
            pltpu.VMEM((cells, nodes, width), BF16),
            pltpu.VMEM((cells, 8, width), F32),
            pltpu.SemaphoreType.DMA((cells,)),
        ]
        + table_scratch,
        compiler_params=params(6),
        cost_estimate=cost(8 * cells * nodes * rank * width, 8 * MIB),
        name="down",
    )(
        table,
        maps,
        edge_map,
        rows,
        node,
        arrived,
        *edges[:-1],
        *part,
        block_split,
        leaf_lift,
        local,
        weighted,
    )
    return adjoint, gradient[0]


def solution(mesh):
    return jax.shard_map(
        shards,
        mesh=mesh,
        in_specs=(
            P(("parts", "loop")),
            P(("parts", "loop"), None, None),
            P(("parts", "loop"), None, None),
            P("parts", None, None, None),
            P("parts", None, None, None),
            P("parts", None, None, None),
            P("parts", None, None, None),
            P("parts", None, None, None),
            P("parts", None, None, None),
            P("parts", None, None, None),
            P("parts", None, None, None),
            P("parts", None, None),
            P("parts", None, None, None),
            P("parts", None, None, None),
            P("parts", None, None),
            P("parts"),
            P("parts"),
            P(),
        ),
        out_specs=(P(("parts", "loop"), None, None), P(("parts", "loop"))),
        check_vma=False,
    )
```
